32 devices in a mesh: groups: 2 (over x), src: 8 (over z, y), tile: 2 (over core).
Axes of the slice: x: 2, y: 2, z: 4, core: 2. Of those that a mesh axis runs over, the one named last changes fastest.
Arguments:
- mask: float32 [2048, 1024], P(('groups', 'tile')), parts along dimension 0, may hold values from 0 to 1
- target: float32 [2048, 1024], P(('groups', 'tile')), parts along dimension 0, may hold values from 0 to 1
- pupil: float32 [64, 64], replicated, may hold values from 0.1 to 1.9
- source_shift: int32 [24, 2], replicated, may hold values from -24 to 24
- source_weight: float32 [24], replicated, may hold values from 0.25 to 4
Outputs:
- mask_gradient: float32 [2048, 1024], P(('groups', 'tile'), 'src'), parts along dimension 0
The draws below stay inside these ranges and needn't reach their ends.
There are 2 independent parts, one for each index of `groups`. The reference program is written for one: setup_inputs(seed, part) draws one part's arguments, and reference() takes and returns one part's arrays. A program takes and returns all parts, laid end to end along the dimension named above; an argument that names none is the same for every part. Nothing has to cross between parts.
Inputs may be any that keep to these rules, and one draw needn't show every extreme that they name: `source_shift`: integer frequency shifts of the source points.
All inputs are finite; a program needn't handle non-finite values.
Results may differ from the reference program's by a relative error of at most 0.0003.
Values sent between devices are 32-bit elements; how exact they have to be, the bound alone decides.
A program may use at most 128 MiB of HBM per device.

```python
import math
import jax
import jax.numpy as jnp
from jax import lax

TS = 512
HALO = 64
K = 64
SRC_DEV = 3
GC = 2
PAD = 640
SOURCES = 24
ROWS = 1024
COLS = 1024
N_SRC = 8
N_TILE = 2


def place_ends(array, key, smallest, high):
    extent = array.shape
    index_at = [jax.random.randint(jax.random.fold_in(key, axis), (), 0, extent[axis]) for axis in range(len(extent))]
    array = array.at[tuple(index_at)].set(smallest)
    longest = extent.index(max(extent))
    index_at[longest] = (index_at[longest] + 1) % extent[longest]
    return array.at[tuple(index_at)].set(high)


def steps_of(own_key, extent, shards, low, largest):
    loudness = 1.0
    for axis_at, blocks in shards:
        draws = jax.random.uniform(jax.random.fold_in(jax.random.fold_in(own_key, 6), axis_at), (blocks,), jnp.float32, low / len(shards), largest / len(shards))
        loudness = loudness * jnp.repeat(jnp.exp(draws), extent[axis_at] // blocks).reshape((-1,) + (1,) * (len(extent) - 1 - axis_at))
    return loudness


def setup_inputs(seed: int = 0, part: int = 0) -> dict:
    splits = jax.random.split(jax.random.key(seed), 6)
    part_keys = jax.random.split(jax.random.fold_in(splits[5], part), 6)
    mask = jnp.clip(1.0 * jax.random.uniform(part_keys[0], (ROWS, COLS), jnp.float32) ** steps_of(part_keys[0], (ROWS, COLS), ((0, 2),), -0.2, 0.2), 0.0, 1.0)
    target = jnp.clip(1.0 * jax.random.uniform(part_keys[1], (ROWS, COLS), jnp.float32) ** steps_of(part_keys[1], (ROWS, COLS), ((0, 2),), -0.2, 0.2), 0.0, 1.0)
    pupil = jnp.clip(1.0 + 0.18 * jax.random.normal(splits[2], (K, K), jnp.float32), 0.1, 1.9)
    source_shift = place_ends(jax.random.randint(splits[3], (SOURCES, 2), -((3 * K) // 8), (3 * K) // 8 + 1), jax.random.fold_in(splits[3], 1), -((3 * K) // 8), ((3 * K) // 8 + 1) - 1).astype(jnp.int32)
    source_weight = jnp.clip(jnp.exp(jax.random.uniform(splits[4], (SOURCES,), jnp.float32, math.log(0.25), math.log(4.0))), 0.25, 4.0)
    return dict(mask=mask, target=target, pupil=pupil, source_shift=source_shift, source_weight=source_weight)


full_turn = 2.0 * math.pi
exact_mode = lax.Precision.HIGHEST
resist_gain = 25.0
resist_level = 0.25

def light_block(tiles, shift_block, weight_block, pupil):
    sources = shift_block.shape[0]
    freqs = pupil.shape[0]
    padded = tiles.shape[1]
    count = tiles.shape[0]
    scaling = full_turn / padded
    centred = jnp.arange(freqs, dtype=jnp.int32) - freqs // 2
    pixels = jnp.arange(padded, dtype=jnp.int32)
    row_freq = centred[None, :] + shift_block[:, 0:1]
    col_freq = centred[None, :] + shift_block[:, 1:2]
    row_phase = jnp.mod(row_freq[:, :, None] * pixels[None, None, :], padded).astype(jnp.float32) * scaling
    col_phase = jnp.mod(col_freq[:, :, None] * pixels[None, None, :], padded).astype(jnp.float32) * scaling
    col_table = jnp.concatenate([jnp.cos(col_phase), -jnp.sin(col_phase)], axis=1)
    col_table = col_table.reshape(sources * 2 * freqs, padded).T
    halfway = jnp.einsum('gxy,yn->gxn', tiles, col_table, precision=exact_mode)
    halfway = halfway.reshape(count, padded, sources, 2 * freqs)
    row_table = jnp.concatenate([jnp.cos(row_phase), jnp.sin(row_phase)], axis=1)
    products = jnp.einsum('sux,gxsn->gsun', row_table, halfway, precision=exact_mode)
    spec_real = (products[:, :, :freqs, :freqs] + products[:, :, freqs:, freqs:]) * pupil
    spec_imag = (products[:, :, :freqs, freqs:] - products[:, :, freqs:, :freqs]) * pupil
    outputs = jnp.arange(TS, dtype=jnp.int32) + HALO
    out_phase = jnp.mod(outputs[:, None] * centred[None, :], padded).astype(jnp.float32) * scaling
    back_cos = jnp.cos(out_phase) / padded
    back_sin = jnp.sin(out_phase) / padded
    back_stack = jnp.concatenate([back_cos, back_sin], axis=0)
    spectra = jnp.concatenate([spec_real, spec_imag], axis=-1)
    mixed = jnp.einsum('xu,gsun->gsxn', back_stack, spectra, precision=exact_mode)
    left_real = mixed[:, :, :TS, :freqs] - mixed[:, :, TS:, freqs:]
    left_imag = mixed[:, :, :TS, freqs:] + mixed[:, :, TS:, :freqs]
    rows_both = jnp.concatenate([left_real, left_imag], axis=-1)
    upper_half = jnp.concatenate([back_cos.T, back_sin.T], axis=1)
    lower_half = jnp.concatenate([-back_sin.T, back_cos.T], axis=1)
    right_table = jnp.concatenate([upper_half, lower_half], axis=0)
    field = jnp.einsum('gsxk,kn->gsxn', rows_both, right_table, precision=exact_mode)
    power = field[..., :TS] * field[..., :TS] + field[..., TS:] * field[..., TS:]
    return lax.optimization_barrier(jnp.sum(power * weight_block[None, :, None, None], axis=1))

def resist_slope(intensity, target):
    printed = jax.nn.sigmoid(resist_gain * (intensity - resist_level))
    return 2.0 * (printed - target) * resist_gain * printed * (1.0 - printed)

def tile_stack(mask_image):
    widened = jnp.pad(mask_image, HALO)
    pieces = []
    for tile_row in range(N_TILE):
        for tile_column in range(GC):
            pieces.append(widened[tile_row * TS:tile_row * TS + PAD, tile_column * TS:tile_column * TS + PAD])
    return jnp.stack(pieces)

def to_image(tiles):
    return tiles.reshape(N_TILE, GC, TS, TS).transpose(0, 2, 1, 3).reshape(N_TILE * TS, GC * TS)

def from_image(image):
    return image.reshape(N_TILE, TS, GC, TS).transpose(0, 2, 1, 3).reshape(N_TILE * GC, TS, TS)

def reference(mask, target, pupil, source_shift, source_weight):
    tiles, unstack = jax.vjp(tile_stack, mask)
    shift_blocks = source_shift.reshape(N_SRC, SRC_DEV, 2)
    weight_blocks = source_weight.reshape(N_SRC, SRC_DEV)
    total_weight = jnp.sum(source_weight)

    def forward_step(carry, block):
        return (carry + light_block(tiles, block[0], block[1], pupil), None)
    start = jnp.zeros((N_TILE * GC, TS, TS), jnp.float32)
    summed, _ = lax.scan(forward_step, start, (shift_blocks, weight_blocks))
    intensity = to_image(summed) / total_weight
    slope_tiles = from_image(resist_slope(intensity, target) / total_weight)

    def backward_step(carry, block):

        def local_light(tile_input):
            return light_block(tile_input, block[0], block[1], pupil)
        _, pullback = jax.vjp(local_light, tiles)
        return (carry + pullback(slope_tiles)[0], None)
    gathered, _ = lax.scan(backward_step, jnp.zeros_like(tiles), (shift_blocks, weight_blocks))
    return unstack(gathered)[0]
```

```python
import numpy as np

import jax
import jax.numpy as jnp
from jax import lax
from jax.sharding import PartitionSpec as P

TS = 512
HALO = 64
PAD = 640
GRID = 128
REACH = 24

exact_mode = lax.Precision.HIGHEST
resist_gain = 25.0
resist_level = 0.25


def tables(freqs, columns):
    pixels = np.arange(PAD)[:, None]
    samples = np.arange(GRID)[None, :] * (PAD // GRID)
    spread = np.ones((PAD, GRID))
    for p in range(1, GRID // 2):
        spread += 2.0 * np.cos(2.0 * np.pi * (p * (pixels - samples) % PAD) / PAD)
    spread /= GRID
    tiles = columns // TS
    across = np.zeros((columns, tiles * GRID))
    for c in range(tiles):
        low, high = max(0, c * TS - HALO), min(columns, c * TS - HALO + PAD)
        across[low:high, c * GRID : (c + 1) * GRID] = spread[low + HALO - c * TS : high + HALO - c * TS]
    bins = np.arange(-freqs // 2 - REACH, freqs // 2 + REACH)[:, None] * np.arange(GRID)[None, :]
    angle = 2.0 * np.pi * (bins % GRID) / GRID
    waves = np.concatenate([np.cos(angle), np.sin(angle)], axis=1)
    return spread, across, waves


def rotation(waves, freqs):
    centre = waves[REACH : REACH + freqs]
    cosine, sine = centre[:, :GRID].T, centre[:, GRID:].T
    return np.block([[cosine, -sine], [sine, cosine]])


def mm(a, b):
    return jnp.dot(a, b, precision=exact_mode, preferred_element_type=jnp.float32)


def resist_slope(intensity, target):
    printed = jax.nn.sigmoid(resist_gain * (intensity - resist_level))
    return 2.0 * (printed - target) * resist_gain * printed * (1.0 - printed)


def halves(y, tiles, freqs):
    real, imag = [], []
    for c in range(tiles):
        top = y[2 * c * freqs : (2 * c + 1) * freqs]
        low = y[(2 * c + 1) * freqs : (2 * c + 2) * freqs]
        real.append(top[:, :GRID] - low[:, GRID:])
        imag.append(top[:, GRID:] + low[:, :GRID])
    return jnp.concatenate(real, axis=1), jnp.concatenate(imag, axis=1)


def shards(mask, target, pupil, source_shift, source_weight):
    f32 = jnp.float32
    me = lax.axis_index("src")
    n = lax.axis_size("src")
    nt = lax.axis_size("tile")
    own = source_shift.shape[0] // n
    freqs = pupil.shape[0]
    columns = mask.shape[1]
    tiles = columns // TS
    width = columns // n
    spread64, across64, waves64 = tables(freqs, columns)
    spread = jnp.asarray(spread64, f32)
    core = spread[HALO : HALO + TS]
    across = jnp.asarray(across64, f32)
    waves = jnp.asarray(waves64, f32)
    fixed = jnp.asarray(waves64[REACH : REACH + freqs], f32)
    turn = jnp.asarray(rotation(waves64, freqs), f32)
    total = jnp.sum(source_weight)
    scaled = jnp.tile(pupil / (PAD * PAD), (2 * tiles, 1))

    above = lax.ppermute(mask[TS - HALO :], "tile", [(i, i + 1) for i in range(nt - 1)])
    below = lax.ppermute(mask[:HALO], "tile", [(i + 1, i) for i in range(nt - 1)])
    strip = jnp.concatenate([above, mask, below], axis=0)
    low = mm(mm(spread.T, strip), across)
    zc = mm(waves[:, :GRID], low)
    zs = mm(waves[:, GRID:], low)
    fields = []
    light = jnp.zeros((GRID, tiles * GRID), f32)
    for s in range(own):
        a = source_shift[me * own + s, 0] + REACH
        b = source_shift[me * own + s, 1] + REACH
        w = source_weight[me * own + s]
        c_rows = lax.dynamic_slice_in_dim(zc, a, freqs, 0)
        s_rows = lax.dynamic_slice_in_dim(zs, a, freqs, 0)
        shifted = lax.dynamic_slice_in_dim(waves, b, freqs, 0)
        rows = []
        for c in range(tiles):
            cc = c_rows[:, c * GRID : (c + 1) * GRID]
            ss = s_rows[:, c * GRID : (c + 1) * GRID]
            rows.append(jnp.concatenate([cc, -ss], axis=1))
            rows.append(jnp.concatenate([-ss, -cc], axis=1))
        spec = mm(jnp.concatenate(rows, axis=0), shifted.T) * scaled
        real, imag = halves(mm(spec, fixed), tiles, freqs)
        field = mm(turn, jnp.concatenate([real, imag], axis=0))
        fields.append(field)
        light = light + w * (field[:GRID] * field[:GRID] + field[GRID:] * field[GRID:])
    light = lax.psum(light, "src")
    up = mm(core, light)
    backs = []
    for c in range(tiles):
        fine = mm(up[:, c * GRID : (c + 1) * GRID], core.T)
        slope = resist_slope(fine / total, target[:, c * TS : (c + 1) * TS]) / total
        backs.append(mm(slope, core))
    pull = mm(core.T, jnp.concatenate(backs, axis=1))
    pull = jnp.concatenate([pull, pull], axis=0)
    grid_grad = jnp.zeros((GRID, tiles * GRID), f32)
    for s in range(own):
        a = source_shift[me * own + s, 0] + REACH
        b = source_shift[me * own + s, 1] + REACH
        w = source_weight[me * own + s]
        shift_a = lax.dynamic_slice_in_dim(waves, a, freqs, 0)
        shift_b = lax.dynamic_slice_in_dim(waves, b, freqs, 0)
        u = mm(turn.T, fields[s] * pull * (2.0 * w))
        rows = []
        for c in range(tiles):
            re = u[:freqs, c * GRID : (c + 1) * GRID]
            im = u[freqs:, c * GRID : (c + 1) * GRID]
            rows.append(jnp.concatenate([re, im], axis=1))
            rows.append(jnp.concatenate([im, -re], axis=1))
        back = mm(jnp.concatenate(rows, axis=0), fixed.T) * scaled
        real, imag = halves(mm(back, shift_b), tiles, freqs)
        grid_grad = grid_grad + mm(shift_a[:, :GRID].T, real) - mm(shift_a[:, GRID:].T, imag)
    grid_grad = lax.psum(grid_grad, "src")
    cols = lax.dynamic_slice_in_dim(across, me * width, width, 0)
    full = mm(spread, mm(grid_grad, cols.T))
    upper, inner, lower = full[:HALO], full[HALO : HALO + TS], full[HALO + TS :]
    from_above = lax.ppermute(lower, "tile", [(i, i + 1) for i in range(nt - 1)])
    from_below = lax.ppermute(upper, "tile", [(i + 1, i) for i in range(nt - 1)])
    inner = inner.at[:HALO].add(from_above)
    return inner.at[TS - HALO :].add(from_below)


def solution(mesh):
    placed = (P(("groups", "tile"), None), P(("groups", "tile"), None), P(), P(), P())
    return jax.shard_map(
        shards, mesh=mesh, in_specs=placed, out_specs=P(("groups", "tile"), "src"), check_vma=False
    )
```

```python
import functools

import numpy as np

import jax
import jax.numpy as jnp
from jax import lax
from jax.experimental import pallas as pl
from jax.experimental.pallas import tpu as pltpu
from jax.sharding import PartitionSpec as P

TS = 512
HALO = 64
PAD = 640
GRID = 128
REACH = 24
CHUNK = 128

MESH = pl.DeviceIdType.MESH
f32, bf16 = jnp.float32, jnp.bfloat16
resist_gain = 25.0
resist_level = 0.25


def tables(freqs, columns):
    pixels = np.arange(PAD)[:, None]
    samples = np.arange(GRID)[None, :] * (PAD // GRID)
    spread = np.ones((PAD, GRID))
    for p in range(1, GRID // 2):
        spread += 2.0 * np.cos(2.0 * np.pi * (p * (pixels - samples) % PAD) / PAD)
    spread /= GRID
    tiles = columns // TS
    across = np.zeros((columns, tiles * GRID))
    for c in range(tiles):
        low, high = max(0, c * TS - HALO), min(columns, c * TS - HALO + PAD)
        across[low:high, c * GRID : (c + 1) * GRID] = spread[low + HALO - c * TS : high + HALO - c * TS]
    bins = np.arange(-freqs // 2 - REACH, freqs // 2 + REACH)[:, None] * np.arange(GRID)[None, :]
    angle = 2.0 * np.pi * (bins % GRID) / GRID
    waves = np.concatenate([np.cos(angle), np.sin(angle)], axis=1)
    return spread, across, waves


def rotation(waves, freqs):
    centre = waves[REACH : REACH + freqs]
    cosine, sine = centre[:, :GRID].T, centre[:, GRID:].T
    return np.block([[cosine, -sine], [sine, cosine]])


def two(array):
    high = array.astype(np.float32).astype(bf16)
    low = (array - high.astype(np.float64)).astype(bf16)
    return np.stack([high, low])


def split(x):
    high = x.astype(bf16)
    return high, (x - high.astype(f32)).astype(bf16)


NN = (((1,), (0,)), ((), ()))
NT = (((1,), (1,)), ((), ()))


def mm(a, b, dims=NN):
    def part(x, y):
        return lax.dot_general(x, y, dims, preferred_element_type=f32)

    return part(a[0], b[0]) + (part(a[0], b[1]) + part(a[1], b[0]))


def pair(ref, *index):
    return ref[(0, *index)], ref[(1, *index)]


def resist_slope(intensity, target):
    printed = jax.nn.sigmoid(resist_gain * (intensity - resist_level))
    return 2.0 * (printed - target) * resist_gain * printed * (1.0 - printed)


def halves(y, tiles, freqs):
    real, imag = [], []
    for c in range(tiles):
        top = y[2 * c * freqs : (2 * c + 1) * freqs]
        low = y[(2 * c + 1) * freqs : (2 * c + 2) * freqs]
        real.append(top[:, :GRID] - low[:, GRID:])
        imag.append(top[:, GRID:] + low[:, :GRID])
    return jnp.concatenate(real, axis=1), jnp.concatenate(imag, axis=1)


def each(count, body):
    if count <= 16:
        for i in range(count):
            body(i)
    else:
        lax.fori_loop(0, count, lambda i, c: (body(i), c)[1], 0)


def kernel(
    n, own, freqs, tiles,
    mask_ref, target_any, pupil_ref, shift_ref, weight_ref,
    core_ref, coret_ref, across_ref, waves_ref, fixed_ref, turn_ref, turnt_ref, edge_ref, edget_ref,
    out_ref,
    target_ref, halo_ref, shifted_ref, low_ref, field_ref, up_ref, pull_ref,
    part_ref, gather_ref, total_ref, rim_ref, rimin_ref,
    target_sem, halo_sem, rim_sem, send_sem, recv_sem,
):
    me = lax.axis_index("src")
    side = lax.axis_index("tile")
    owners = part_ref.shape[1]
    held = part_ref.shape[2]
    width = out_ref.shape[1]
    spans = tiles * GRID

    fetch = pltpu.make_async_copy(target_any, target_ref, target_sem)
    fetch.start()

    barrier = pltpu.get_barrier_semaphore()
    pl.semaphore_signal(barrier, inc=1, device_id={"tile": 1 - side}, device_id_type=MESH)

    def greet(i):
        pl.semaphore_signal(barrier, inc=1, device_id={"src": lax.rem(me + i + 1, n)}, device_id_type=MESH)

    each(n - 1, greet)

    span = waves_ref.shape[1]
    gap = lax.broadcasted_iota(jnp.int32, (freqs, span), 1) - lax.broadcasted_iota(jnp.int32, (freqs, span), 0)
    for s in range(own):
        for axis in (0, 1):
            picks = jnp.where(gap == shift_ref[me * own + s, axis] + REACH, 1.0, 0.0).astype(bf16)
            shifted_ref[s, axis] = lax.dot_general(picks, waves_ref[0], NN, preferred_element_type=f32) + lax.dot_general(
                picks, waves_ref[1], NN, preferred_element_type=f32
            )

    low_ref[...] = jnp.zeros_like(low_ref)

    def project(left, source, height):
        def block(i, carry):
            at = pl.multiple_of(i * 256, 256)
            rows = mm(left, split(source[0:height, pl.ds(at, 256)]))
            low_ref[...] += mm(split(rows), pair(across_ref, pl.ds(at, 256)))
            return carry

        lax.fori_loop(0, mask_ref.shape[1] // 256, block, 0)

    pl.semaphore_wait(barrier, n)
    first = pl.multiple_of((TS - HALO) * (1 - side), HALO)
    halo = pltpu.make_async_remote_copy(
        src_ref=mask_ref.at[pl.ds(first, HALO)],
        dst_ref=halo_ref,
        send_sem=halo_sem.at[0],
        recv_sem=halo_sem.at[1],
        device_id={"tile": 1 - side},
        device_id_type=MESH,
    )
    halo.start()
    project(pair(coret_ref), mask_ref, TS)
    halo.wait_recv()
    project(pair(edget_ref, side), halo_ref, HALO)

    low = split(low_ref[...])

    def turns():
        return jnp.concatenate(
            [shifted_ref[s, 0, :, half * GRID : (half + 1) * GRID] for s in range(own) for half in (0, 1)], axis=0
        )

    spun = mm(split(turns()), low)
    scaled = pupil_ref[...] * (1.0 / (PAD * PAD))
    scaled = jnp.concatenate([scaled] * (2 * tiles), axis=0)
    fixed = pair(fixed_ref)

    light = jnp.zeros((GRID, spans), f32)
    for s in range(own):
        w = weight_ref[me * own + s]
        c_rows = spun[2 * s * freqs : (2 * s + 1) * freqs]
        s_rows = spun[(2 * s + 1) * freqs : (2 * s + 2) * freqs]
        rows = []
        for c in range(tiles):
            cc = c_rows[:, c * GRID : (c + 1) * GRID]
            ss = s_rows[:, c * GRID : (c + 1) * GRID]
            rows.append(jnp.concatenate([cc, -ss], axis=1))
            rows.append(jnp.concatenate([-ss, -cc], axis=1))
        spec = mm(split(jnp.concatenate(rows, axis=0)), split(shifted_ref[s, 1]), NT) * scaled
        real, imag = halves(mm(split(spec), fixed), tiles, freqs)
        field = mm(pair(turn_ref), split(jnp.concatenate([real, imag], axis=0)))
        field_ref[s] = field
        light = light + w * (field[:GRID] * field[:GRID] + field[GRID:] * field[GRID:])

    def summed(k, value):
        for p in range(owners):
            part_ref[k, p] = value[p * held : (p + 1) * held]

        def owning(condition, action):
            if owners == n:
                action()
            else:
                pl.when(condition)(action)

        def scatter(peer):
            return pltpu.make_async_remote_copy(
                src_ref=part_ref.at[k, lax.rem(peer, owners)],
                dst_ref=gather_ref.at[k, me],
                send_sem=send_sem.at[2 * k, peer],
                recv_sem=recv_sem.at[2 * k, me],
                device_id={"src": peer},
                device_id_type=MESH,
            )

        def arrival(peer):
            return pltpu.make_async_remote_copy(
                src_ref=part_ref.at[k, 0],
                dst_ref=gather_ref.at[k, peer],
                send_sem=send_sem.at[2 * k, peer],
                recv_sem=recv_sem.at[2 * k, peer],
                device_id={"src": peer},
                device_id_type=MESH,
            )

        def share(peer):
            return pltpu.make_async_remote_copy(
                src_ref=total_ref.at[k, lax.rem(me, owners)],
                dst_ref=total_ref.at[k, lax.rem(me, owners)],
                send_sem=send_sem.at[2 * k + 1, peer],
                recv_sem=recv_sem.at[2 * k + 1, me],
                device_id={"src": peer},
                device_id_type=MESH,
            )

        def shared(peer):
            return pltpu.make_async_remote_copy(
                src_ref=total_ref.at[k, lax.rem(peer, owners)],
                dst_ref=total_ref.at[k, lax.rem(peer, owners)],
                send_sem=send_sem.at[2 * k + 1, peer],
                recv_sem=recv_sem.at[2 * k + 1, peer],
                device_id={"src": peer},
                device_id_type=MESH,
            )

        def other(i):
            return lax.rem(me + i + 1, n)

        each(n - 1, lambda i: owning(other(i) < owners, lambda: scatter(other(i)).start()))

        def add_up():
            each(n - 1, lambda i: arrival(other(i)).wait_recv())
            gather_ref[k, me] = part_ref[k, lax.rem(me, owners)]
            block = gather_ref[k, 0]
            if n <= 16:
                for p in range(1, n):
                    block = block + gather_ref[k, p]
            else:
                block = lax.fori_loop(1, n, lambda p, t: t + gather_ref[k, p], block)
            total_ref[k, lax.rem(me, owners)] = block
            each(n - 1, lambda i: share(other(i)).start())

        owning(me < owners, add_up)
        each(n - 1, lambda i: owning(other(i) < owners, lambda: shared(other(i)).wait_recv()))
        each(n - 1, lambda i: owning(other(i) < owners, lambda: scatter(other(i)).wait_send()))
        owning(me < owners, lambda: each(n - 1, lambda i: share(other(i)).wait_send()))
        return jnp.concatenate([total_ref[k, p] for p in range(owners)], axis=0)

    light = split(summed(0, light))

    weight = weight_ref[0]
    for s in range(1, n * own):
        weight = weight + weight_ref[s]
    inverse = 1.0 / jnp.full((1, TS), weight, f32)
    fetch.wait()
    core = pair(core_ref)
    coret = pair(coret_ref)
    up_ref[...] = mm(core, light)
    pull_ref[...] = jnp.zeros_like(pull_ref)

    def resist(i, carry):
        at = pl.multiple_of(i * CHUNK, CHUNK)
        backs = []
        for c in range(tiles):
            fine = mm(split(up_ref[pl.ds(at, CHUNK), c * GRID : (c + 1) * GRID]), coret)
            slope = resist_slope(fine * inverse, target_ref[pl.ds(at, CHUNK), c * TS : (c + 1) * TS]) * inverse
            backs.append(mm(split(slope), core))
        rows = jnp.concatenate(backs, axis=1)
        pull_ref[...] += mm(pair(coret_ref, slice(None), pl.ds(at, CHUNK)), split(rows))
        return carry

    lax.fori_loop(0, TS // CHUNK, resist, 0)

    pull = jnp.concatenate([pull_ref[...]] * 2, axis=0)
    lows = []
    for s in range(own):
        w = weight_ref[me * own + s]
        u = mm(pair(turnt_ref), split(field_ref[s] * pull * (2.0 * w)))
        rows = []
        for c in range(tiles):
            re = u[:freqs, c * GRID : (c + 1) * GRID]
            im = u[freqs:, c * GRID : (c + 1) * GRID]
            rows.append(jnp.concatenate([re, im], axis=1))
            rows.append(jnp.concatenate([im, -re], axis=1))
        back = mm(split(jnp.concatenate(rows, axis=0)), fixed, NT) * scaled
        real, imag = halves(mm(split(back), split(shifted_ref[s, 1])), tiles, freqs)
        lows += [real, -imag]
    lead = split(turns().T)
    grid_grad = mm(lead, split(jnp.concatenate(lows, axis=0)))

    grid_grad = split(summed(1, grid_grad))
    at = pl.multiple_of(me * width, width)
    block = split(mm(grid_grad, pair(across_ref, pl.ds(at, width)), NT))
    rim_ref[...] = mm(pair(edge_ref, side), block)
    rim = pltpu.make_async_remote_copy(
        src_ref=rim_ref,
        dst_ref=rimin_ref,
        send_sem=rim_sem.at[0],
        recv_sem=rim_sem.at[1],
        device_id={"tile": 1 - side},
        device_id_type=MESH,
    )
    rim.start()
    out_ref[...] = mm(core, block)
    rim.wait_recv()
    out_ref[pl.ds(first, HALO), :] += rimin_ref[...]
    halo.wait_send()
    rim.wait_send()


def shards(mask, target, pupil, source_shift, source_weight):
    n = lax.axis_size("src")
    assert lax.axis_size("tile") == 2
    own = source_shift.shape[0] // n
    freqs = pupil.shape[0]
    columns = mask.shape[1]
    tiles = columns // TS
    width = columns // n
    owners = min(n, GRID // 8)
    spans = tiles * GRID
    spread, across, waves = tables(freqs, columns)
    core = spread[HALO : HALO + TS]
    edges = np.stack([spread[HALO + TS :], spread[:HALO]])
    turn = rotation(waves, freqs)
    constants = [
        two(core), two(core.T), two(across), two(waves),
        two(waves[REACH : REACH + freqs]), two(turn), two(turn.T), two(edges), two(edges.transpose(0, 2, 1)),
    ]
    vmem = pl.BlockSpec(memory_space=pltpu.VMEM)
    smem = pl.BlockSpec(memory_space=pltpu.SMEM)
    return pl.pallas_call(
        functools.partial(kernel, n, own, freqs, tiles),
        out_shape=jax.ShapeDtypeStruct((TS, width), f32),
        in_specs=[vmem, pl.BlockSpec(memory_space=pl.ANY), vmem, smem, smem] + [vmem] * len(constants),
        out_specs=vmem,
        scratch_shapes=[
            pltpu.VMEM((TS, columns), f32),
            pltpu.VMEM((HALO, columns), f32),
            pltpu.VMEM((own, 2, freqs, 2 * GRID), f32),
            pltpu.VMEM((GRID, spans), f32),
            pltpu.VMEM((own, 2 * GRID, spans), f32),
            pltpu.VMEM((TS, spans), f32),
            pltpu.VMEM((GRID, spans), f32),
            pltpu.VMEM((2, owners, GRID // owners, spans), f32),
            pltpu.VMEM((2, n, GRID // owners, spans), f32),
            pltpu.VMEM((2, owners, GRID // owners, spans), f32),
            pltpu.VMEM((HALO, width), f32),
            pltpu.VMEM((HALO, width), f32),
            pltpu.SemaphoreType.DMA,
            pltpu.SemaphoreType.DMA((2,)),
            pltpu.SemaphoreType.DMA((2,)),
            pltpu.SemaphoreType.DMA((4, n)),
            pltpu.SemaphoreType.DMA((4, n)),
        ],
        compiler_params=pltpu.CompilerParams(
            collective_id=0, has_side_effects=True, vmem_limit_bytes=60 * 1024 * 1024
        ),
    )(mask, target, pupil, source_shift, source_weight, *[jnp.asarray(c) for c in constants])


def solution(mesh):
    placed = (P(("groups", "tile"), None), P(("groups", "tile"), None), P(), P(), P())
    return jax.shard_map(
        shards, mesh=mesh, in_specs=placed, out_specs=P(("groups", "tile"), "src"), check_vma=False
    )
```

```python
import functools

import numpy as np

import jax
import jax.numpy as jnp
from jax import lax
from jax.experimental import pallas as pl
from jax.experimental.pallas import tpu as pltpu
from jax.sharding import PartitionSpec as P

TS = 512
HALO = 64
PAD = 640
GRID = 128
REACH = 24
CHUNK = 128

MESH = pl.DeviceIdType.MESH
f32, bf16 = jnp.float32, jnp.bfloat16
resist_gain = 25.0
resist_level = 0.25


def tables(freqs, columns):
    pixels = np.arange(PAD)[:, None]
    samples = np.arange(GRID)[None, :] * (PAD // GRID)
    spread = np.ones((PAD, GRID))
    for p in range(1, GRID // 2):
        spread += 2.0 * np.cos(2.0 * np.pi * (p * (pixels - samples) % PAD) / PAD)
    spread /= GRID
    tiles = columns // TS
    across = np.zeros((columns, tiles * GRID))
    for c in range(tiles):
        low, high = max(0, c * TS - HALO), min(columns, c * TS - HALO + PAD)
        across[low:high, c * GRID : (c + 1) * GRID] = spread[low + HALO - c * TS : high + HALO - c * TS]
    bins = np.arange(-freqs // 2 - REACH, freqs // 2 + REACH)[:, None] * np.arange(GRID)[None, :]
    angle = 2.0 * np.pi * (bins % GRID) / GRID
    waves = np.concatenate([np.cos(angle), np.sin(angle)], axis=1)
    return spread, across, waves


def rotation(waves, freqs):
    centre = waves[REACH : REACH + freqs]
    cosine, sine = centre[:, :GRID].T, centre[:, GRID:].T
    return np.block([[cosine, -sine], [sine, cosine]])


def two(array):
    high = array.astype(np.float32).astype(bf16)
    low = (array - high.astype(np.float64)).astype(bf16)
    return np.stack([high, low])


def split(x):
    high = x.astype(bf16)
    return high, (x - high.astype(f32)).astype(bf16)


NN = (((1,), (0,)), ((), ()))
NT = (((1,), (1,)), ((), ()))


def mm(a, b, dims=NN):
    def part(x, y):
        return lax.dot_general(x, y, dims, preferred_element_type=f32)

    return part(a[0], b[0]) + (part(a[0], b[1]) + part(a[1], b[0]))


def pair(ref, *index):
    return ref[(0, *index)], ref[(1, *index)]


def resist_slope(intensity, target):
    printed = jax.nn.sigmoid(resist_gain * (intensity - resist_level))
    return 2.0 * (printed - target) * resist_gain * printed * (1.0 - printed)


def halves(y, tiles, freqs):
    real, imag = [], []
    for c in range(tiles):
        top = y[2 * c * freqs : (2 * c + 1) * freqs]
        low = y[(2 * c + 1) * freqs : (2 * c + 2) * freqs]
        real.append(top[:, :GRID] - low[:, GRID:])
        imag.append(top[:, GRID:] + low[:, :GRID])
    return jnp.concatenate(real, axis=1), jnp.concatenate(imag, axis=1)


def each(count, body):
    if count <= 16:
        for i in range(count):
            body(i)
    else:
        lax.fori_loop(0, count, lambda i, c: (body(i), c)[1], 0)


def kernel(
    n, own, freqs, tiles,
    mask_any, target_any, pupil_ref, shift_ref, weight_ref,
    core_any, coret_any, across_any, waves_any, fixed_any, turn_any, turnt_any, edge_any, edget_any,
    out_ref,
    core_ref, coret_ref, across_ref, waves_ref, fixed_ref, turn_ref, turnt_ref, edge_ref, edget_ref,
    mask_ref, target_ref, halo_ref, shifted_ref, low_ref, field_ref, up_ref, pull_ref,
    part_ref, gather_ref, total_ref, rim_ref, rimin_ref,
    load_sem, halo_sem, rim_sem, send_sem, recv_sem,
):
    me = lax.axis_index("src")
    side = lax.axis_index("tile")
    owners = part_ref.shape[1]
    held = part_ref.shape[2]
    width = out_ref.shape[1]
    spans = tiles * GRID

    barrier = pltpu.get_barrier_semaphore()
    pl.semaphore_signal(barrier, inc=1, device_id={"tile": 1 - side}, device_id_type=MESH)

    def greet(i):
        pl.semaphore_signal(barrier, inc=1, device_id={"src": lax.rem(me + i + 1, n)}, device_id_type=MESH)

    each(n - 1, greet)

    places = [
        (waves_any, waves_ref), (mask_any, mask_ref), (coret_any, coret_ref), (across_any, across_ref),
        (edget_any, edget_ref), (fixed_any, fixed_ref), (turn_any, turn_ref), (target_any, target_ref),
        (core_any, core_ref), (turnt_any, turnt_ref), (edge_any, edge_ref),
    ]
    loads = [pltpu.make_async_copy(source, place, load_sem.at[i]) for i, (source, place) in enumerate(places)]
    for load in loads:
        load.start()
    loads[0].wait()

    span = waves_ref.shape[1]
    gap = lax.broadcasted_iota(jnp.int32, (freqs, span), 1) - lax.broadcasted_iota(jnp.int32, (freqs, span), 0)
    for s in range(own):
        for axis in (0, 1):
            picks = jnp.where(gap == shift_ref[axis, me * own + s] + REACH, 1.0, 0.0).astype(bf16)
            shifted_ref[s, axis] = lax.dot_general(picks, waves_ref[0], NN, preferred_element_type=f32) + lax.dot_general(
                picks, waves_ref[1], NN, preferred_element_type=f32
            )

    low_ref[...] = jnp.zeros_like(low_ref)

    def project(left, source, height):
        def block(i, carry):
            at = pl.multiple_of(i * 256, 256)
            rows = mm(left, split(source[0:height, pl.ds(at, 256)]))
            low_ref[...] += mm(split(rows), pair(across_ref, pl.ds(at, 256)))
            return carry

        lax.fori_loop(0, mask_ref.shape[1] // 256, block, 0)

    pl.semaphore_wait(barrier, n)
    first = pl.multiple_of((TS - HALO) * (1 - side), HALO)
    halo = pltpu.make_async_remote_copy(
        src_ref=mask_any.at[pl.ds(first, HALO)],
        dst_ref=halo_ref,
        send_sem=halo_sem.at[0],
        recv_sem=halo_sem.at[1],
        device_id={"tile": 1 - side},
        device_id_type=MESH,
    )
    halo.start()
    for load in loads[1:4]:
        load.wait()
    project(pair(coret_ref), mask_ref, TS)
    for load in loads[4:7]:
        load.wait()
    halo.wait_recv()
    project(pair(edget_ref, side), halo_ref, HALO)

    low = split(low_ref[...])

    def turns():
        return jnp.concatenate(
            [shifted_ref[s, 0, :, half * GRID : (half + 1) * GRID] for s in range(own) for half in (0, 1)], axis=0
        )

    spun = mm(split(turns()), low)
    scaled = pupil_ref[...] * (1.0 / (PAD * PAD))
    scaled = jnp.concatenate([scaled] * (2 * tiles), axis=0)
    fixed = pair(fixed_ref)

    light = jnp.zeros((GRID, spans), f32)
    for s in range(own):
        w = weight_ref[me * own + s]
        c_rows = spun[2 * s * freqs : (2 * s + 1) * freqs]
        s_rows = spun[(2 * s + 1) * freqs : (2 * s + 2) * freqs]
        rows = []
        for c in range(tiles):
            cc = c_rows[:, c * GRID : (c + 1) * GRID]
            ss = s_rows[:, c * GRID : (c + 1) * GRID]
            rows.append(jnp.concatenate([cc, -ss], axis=1))
            rows.append(jnp.concatenate([-ss, -cc], axis=1))
        spec = mm(split(jnp.concatenate(rows, axis=0)), split(shifted_ref[s, 1]), NT) * scaled
        real, imag = halves(mm(split(spec), fixed), tiles, freqs)
        field = mm(pair(turn_ref), split(jnp.concatenate([real, imag], axis=0)))
        field_ref[s] = field
        light = light + w * (field[:GRID] * field[:GRID] + field[GRID:] * field[GRID:])

    def summed(k, value):
        for p in range(owners):
            part_ref[k, p] = value[p * held : (p + 1) * held]

        def owning(condition, action):
            if owners == n:
                action()
            else:
                pl.when(condition)(action)

        def scatter(peer):
            return pltpu.make_async_remote_copy(
                src_ref=part_ref.at[k, lax.rem(peer, owners)],
                dst_ref=gather_ref.at[k, me],
                send_sem=send_sem.at[2 * k, peer],
                recv_sem=recv_sem.at[2 * k, me],
                device_id={"src": peer},
                device_id_type=MESH,
            )

        def arrival(peer):
            return pltpu.make_async_remote_copy(
                src_ref=part_ref.at[k, 0],
                dst_ref=gather_ref.at[k, peer],
                send_sem=send_sem.at[2 * k, peer],
                recv_sem=recv_sem.at[2 * k, peer],
                device_id={"src": peer},
                device_id_type=MESH,
            )

        def share(peer):
            return pltpu.make_async_remote_copy(
                src_ref=total_ref.at[k, lax.rem(me, owners)],
                dst_ref=total_ref.at[k, lax.rem(me, owners)],
                send_sem=send_sem.at[2 * k + 1, peer],
                recv_sem=recv_sem.at[2 * k + 1, me],
                device_id={"src": peer},
                device_id_type=MESH,
            )

        def shared(peer):
            return pltpu.make_async_remote_copy(
                src_ref=total_ref.at[k, lax.rem(peer, owners)],
                dst_ref=total_ref.at[k, lax.rem(peer, owners)],
                send_sem=send_sem.at[2 * k + 1, peer],
                recv_sem=recv_sem.at[2 * k + 1, peer],
                device_id={"src": peer},
                device_id_type=MESH,
            )

        def other(i):
            return lax.rem(me + i + 1, n)

        each(n - 1, lambda i: owning(other(i) < owners, lambda: scatter(other(i)).start()))

        def add_up():
            each(n - 1, lambda i: arrival(other(i)).wait_recv())
            gather_ref[k, me] = part_ref[k, lax.rem(me, owners)]
            block = gather_ref[k, 0]
            if n <= 16:
                for p in range(1, n):
                    block = block + gather_ref[k, p]
            else:
                block = lax.fori_loop(1, n, lambda p, t: t + gather_ref[k, p], block)
            total_ref[k, lax.rem(me, owners)] = block
            each(n - 1, lambda i: share(other(i)).start())

        owning(me < owners, add_up)
        each(n - 1, lambda i: owning(other(i) < owners, lambda: shared(other(i)).wait_recv()))
        each(n - 1, lambda i: owning(other(i) < owners, lambda: scatter(other(i)).wait_send()))
        owning(me < owners, lambda: each(n - 1, lambda i: share(other(i)).wait_send()))
        return jnp.concatenate([total_ref[k, p] for p in range(owners)], axis=0)

    light = split(summed(0, light))

    weight = weight_ref[0]
    for s in range(1, n * own):
        weight = weight + weight_ref[s]
    inverse = 1.0 / jnp.full((1, TS), weight, f32)
    for load in loads[7:]:
        load.wait()
    core = pair(core_ref)
    coret = pair(coret_ref)
    up_ref[...] = mm(core, light)
    pull_ref[...] = jnp.zeros_like(pull_ref)

    def resist(i, carry):
        at = pl.multiple_of(i * CHUNK, CHUNK)
        backs = []
        for c in range(tiles):
            fine = mm(split(up_ref[pl.ds(at, CHUNK), c * GRID : (c + 1) * GRID]), coret)
            slope = resist_slope(fine * inverse, target_ref[pl.ds(at, CHUNK), c * TS : (c + 1) * TS]) * inverse
            backs.append(mm(split(slope), core))
        rows = jnp.concatenate(backs, axis=1)
        pull_ref[...] += mm(pair(coret_ref, slice(None), pl.ds(at, CHUNK)), split(rows))
        return carry

    lax.fori_loop(0, TS // CHUNK, resist, 0)

    pull = jnp.concatenate([pull_ref[...]] * 2, axis=0)
    lows = []
    for s in range(own):
        w = weight_ref[me * own + s]
        u = mm(pair(turnt_ref), split(field_ref[s] * pull * (2.0 * w)))
        rows = []
        for c in range(tiles):
            re = u[:freqs, c * GRID : (c + 1) * GRID]
            im = u[freqs:, c * GRID : (c + 1) * GRID]
            rows.append(jnp.concatenate([re, im], axis=1))
            rows.append(jnp.concatenate([im, -re], axis=1))
        back = mm(split(jnp.concatenate(rows, axis=0)), fixed, NT) * scaled
        real, imag = halves(mm(split(back), split(shifted_ref[s, 1])), tiles, freqs)
        lows += [real, -imag]
    lead = split(turns().T)
    grid_grad = mm(lead, split(jnp.concatenate(lows, axis=0)))

    grid_grad = split(summed(1, grid_grad))
    at = pl.multiple_of(me * width, width)
    block = split(mm(grid_grad, pair(across_ref, pl.ds(at, width)), NT))
    rim_ref[...] = mm(pair(edge_ref, side), block)
    rim = pltpu.make_async_remote_copy(
        src_ref=rim_ref,
        dst_ref=rimin_ref,
        send_sem=rim_sem.at[0],
        recv_sem=rim_sem.at[1],
        device_id={"tile": 1 - side},
        device_id_type=MESH,
    )
    rim.start()
    out_ref[...] = mm(core, block)
    rim.wait_recv()
    out_ref[pl.ds(first, HALO), :] += rimin_ref[...]
    halo.wait_send()
    rim.wait_send()


def shards(mask, target, pupil, source_shift, source_weight):
    n = lax.axis_size("src")
    assert lax.axis_size("tile") == 2
    own = source_shift.shape[0] // n
    freqs = pupil.shape[0]
    columns = mask.shape[1]
    tiles = columns // TS
    width = columns // n
    owners = min(n, GRID // 8)
    spans = tiles * GRID
    spread, across, waves = tables(freqs, columns)
    core = spread[HALO : HALO + TS]
    edges = np.stack([spread[HALO + TS :], spread[:HALO]])
    turn = rotation(waves, freqs)
    constants = [
        two(core), two(core.T), two(across), two(waves),
        two(waves[REACH : REACH + freqs]), two(turn), two(turn.T), two(edges), two(edges.transpose(0, 2, 1)),
    ]
    hbm = pl.BlockSpec(memory_space=pl.ANY)
    vmem = pl.BlockSpec(memory_space=pltpu.VMEM)
    smem = pl.BlockSpec(memory_space=pltpu.SMEM)
    return pl.pallas_call(
        functools.partial(kernel, n, own, freqs, tiles),
        out_shape=jax.ShapeDtypeStruct((TS, width), f32),
        in_specs=[hbm, hbm, vmem, smem, smem] + [hbm] * len(constants),
        out_specs=vmem,
        scratch_shapes=[pltpu.VMEM(c.shape, c.dtype) for c in constants] + [
            pltpu.VMEM((TS, columns), f32),
            pltpu.VMEM((TS, columns), f32),
            pltpu.VMEM((HALO, columns), f32),
            pltpu.VMEM((own, 2, freqs, 2 * GRID), f32),
            pltpu.VMEM((GRID, spans), f32),
            pltpu.VMEM((own, 2 * GRID, spans), f32),
            pltpu.VMEM((TS, spans), f32),
            pltpu.VMEM((GRID, spans), f32),
            pltpu.VMEM((2, owners, GRID // owners, spans), f32),
            pltpu.VMEM((2, n, GRID // owners, spans), f32),
            pltpu.VMEM((2, owners, GRID // owners, spans), f32),
            pltpu.VMEM((HALO, width), f32),
            pltpu.VMEM((HALO, width), f32),
            pltpu.SemaphoreType.DMA((2 + len(constants),)),
            pltpu.SemaphoreType.DMA((2,)),
            pltpu.SemaphoreType.DMA((2,)),
            pltpu.SemaphoreType.DMA((4, n)),
            pltpu.SemaphoreType.DMA((4, n)),
        ],
        compiler_params=pltpu.CompilerParams(
            collective_id=0, has_side_effects=True, vmem_limit_bytes=60 * 1024 * 1024
        ),
    )(mask, target, pupil, source_shift.T, source_weight, *[jnp.asarray(c) for c in constants])


def solution(mesh):
    placed = (P(("groups", "tile"), None), P(("groups", "tile"), None), P(), P(), P())
    return jax.shard_map(
        shards, mesh=mesh, in_specs=placed, out_specs=P(("groups", "tile"), "src"), check_vma=False
    )
```

```python
import functools

import numpy as np

import jax
import jax.numpy as jnp
from jax import lax
from jax.experimental import pallas as pl
from jax.experimental.pallas import tpu as pltpu
from jax.sharding import PartitionSpec as P

TS = 512
HALO = 64
PAD = 640
GRID = 128
REACH = 24
CHUNK = 256

MESH = pl.DeviceIdType.MESH
f32, bf16 = jnp.float32, jnp.bfloat16
resist_gain = 25.0
resist_level = 0.25


def tables(freqs, columns):
    pixels = np.arange(PAD)[:, None]
    samples = np.arange(GRID)[None, :] * (PAD // GRID)
    spread = np.ones((PAD, GRID))
    for p in range(1, GRID // 2):
        spread += 2.0 * np.cos(2.0 * np.pi * (p * (pixels - samples) % PAD) / PAD)
    spread /= GRID
    tiles = columns // TS
    across = np.zeros((columns, tiles * GRID))
    for c in range(tiles):
        low, high = max(0, c * TS - HALO), min(columns, c * TS - HALO + PAD)
        across[low:high, c * GRID : (c + 1) * GRID] = spread[low + HALO - c * TS : high + HALO - c * TS]
    bins = np.arange(-freqs // 2 - REACH, freqs // 2 + REACH)[:, None] * np.arange(GRID)[None, :]
    angle = 2.0 * np.pi * (bins % GRID) / GRID
    waves = np.concatenate([np.cos(angle), np.sin(angle)], axis=1)
    return spread, across, waves


def rotation(waves, freqs):
    centre = waves[REACH : REACH + freqs]
    cosine, sine = centre[:, :GRID].T, centre[:, GRID:].T
    return np.block([[cosine, -sine], [sine, cosine]])


def two(array):
    high = array.astype(np.float32).astype(bf16)
    low = (array - high.astype(np.float64)).astype(bf16)
    return np.stack([high, low])


def split(x):
    high = x.astype(bf16)
    return high, (x - high.astype(f32)).astype(bf16)


NN = (((1,), (0,)), ((), ()))
NT = (((1,), (1,)), ((), ()))


def mm(a, b, dims=NN):
    def part(x, y):
        return lax.dot_general(x, y, dims, preferred_element_type=f32)

    return part(a[0], b[0]) + (part(a[0], b[1]) + part(a[1], b[0]))


def pair(ref, *index):
    return ref[(0, *index)], ref[(1, *index)]


def resist_slope(intensity, target):
    printed = jax.nn.sigmoid(resist_gain * (intensity - resist_level))
    return 2.0 * (printed - target) * resist_gain * printed * (1.0 - printed)


def halves(y, count, freqs):
    real, imag = [], []
    for c in range(count):
        top = y[2 * c * freqs : (2 * c + 1) * freqs]
        low = y[(2 * c + 1) * freqs : (2 * c + 2) * freqs]
        real.append(top[:, :GRID] - low[:, GRID:])
        imag.append(top[:, GRID:] + low[:, :GRID])
    return real, imag


def each(count, body):
    if count <= 16:
        for i in range(count):
            body(i)
    else:
        lax.fori_loop(0, count, lambda i, c: (body(i), c)[1], 0)


def kernel(
    n, own, freqs, tiles,
    mask_any, target_any, pupil_ref, shift_ref, weight_ref,
    core_any, coret_any, across_any, waves_any, fixed_any, turn_any, turnt_any, edge_any, edget_any,
    out_ref,
    core_ref, coret_ref, across_ref, waves_ref, fixed_ref, turn_ref, turnt_ref, edge_ref, edget_ref,
    mask_ref, target_ref, halo_ref, shifted_ref, low_ref, field_ref, up_ref, pull_ref,
    part_ref, gather_ref, total_ref, rim_ref, rimin_ref,
    load_sem, halo_sem, rim_sem, send_sem, recv_sem,
):
    me = lax.axis_index("src")
    side = lax.axis_index("tile")
    owners = part_ref.shape[1]
    held = part_ref.shape[2]
    width = out_ref.shape[1]

    barrier = pltpu.get_barrier_semaphore()
    pl.semaphore_signal(barrier, inc=1, device_id={"tile": 1 - side}, device_id_type=MESH)

    def greet(i):
        pl.semaphore_signal(barrier, inc=1, device_id={"src": lax.rem(me + i + 1, n)}, device_id_type=MESH)

    each(n - 1, greet)

    places = [
        (waves_any, waves_ref), (mask_any, mask_ref), (coret_any, coret_ref), (across_any, across_ref),
        (edget_any, edget_ref), (fixed_any, fixed_ref), (turn_any, turn_ref), (target_any, target_ref),
        (core_any, core_ref), (turnt_any, turnt_ref), (edge_any, edge_ref),
    ]
    loads = [pltpu.make_async_copy(source, place, load_sem.at[i]) for i, (source, place) in enumerate(places)]
    for load in loads:
        load.start()
    loads[0].wait()

    span = waves_ref.shape[1]
    gap = lax.broadcasted_iota(jnp.int32, (freqs, span), 1) - lax.broadcasted_iota(jnp.int32, (freqs, span), 0)
    for s in range(own):
        for axis in (0, 1):
            picks = jnp.where(gap == shift_ref[axis, me * own + s] + REACH, 1.0, 0.0).astype(bf16)
            shifted_ref[s, axis] = lax.dot_general(picks, waves_ref[0], NN, preferred_element_type=f32) + lax.dot_general(
                picks, waves_ref[1], NN, preferred_element_type=f32
            )

    low_ref[...] = jnp.zeros_like(low_ref)

    def project(left, source, height):
        def block(i, carry):
            at = pl.multiple_of(i * 256, 256)
            rows = mm(left, split(source[0:height, pl.ds(at, 256)]))
            low_ref[...] += mm(split(rows), pair(across_ref, pl.ds(at, 256)))
            return carry

        lax.fori_loop(0, mask_ref.shape[1] // 256, block, 0)

    pl.semaphore_wait(barrier, n)
    first = pl.multiple_of((TS - HALO) * (1 - side), HALO)
    halo = pltpu.make_async_remote_copy(
        src_ref=mask_any.at[pl.ds(first, HALO)],
        dst_ref=halo_ref,
        send_sem=halo_sem.at[0],
        recv_sem=halo_sem.at[1],
        device_id={"tile": 1 - side},
        device_id_type=MESH,
    )
    halo.start()
    for load in loads[1:4]:
        load.wait()
    project(pair(coret_ref), mask_ref, TS)
    for load in loads[4:7]:
        load.wait()
    halo.wait_recv()
    project(pair(edget_ref, side), halo_ref, HALO)

    low = split(low_ref[...])

    def turns():
        return jnp.concatenate(
            [shifted_ref[s, 0, :, half * GRID : (half + 1) * GRID] for s in range(own) for half in (0, 1)], axis=0
        )

    spun = mm(split(turns()), low)
    scaled = pupil_ref[...] * (1.0 / (PAD * PAD))
    scaled = jnp.concatenate([scaled] * (2 * own), axis=0)
    fixed = pair(fixed_ref)

    weights = [weight_ref[me * own + s] for s in range(own)]

    def image(c):
        lanes = slice(c * GRID, (c + 1) * GRID)
        specs = []
        for s in range(own):
            cc = spun[2 * s * freqs : (2 * s + 1) * freqs, lanes]
            ss = spun[(2 * s + 1) * freqs : (2 * s + 2) * freqs, lanes]
            rows = [jnp.concatenate([cc, -ss], axis=1), jnp.concatenate([-ss, -cc], axis=1)]
            specs.append(mm(split(jnp.concatenate(rows, axis=0)), split(shifted_ref[s, 1]), NT))
        spec = jnp.concatenate(specs, axis=0) * scaled
        real, imag = halves(mm(split(spec), fixed), own, freqs)
        stack = jnp.concatenate([jnp.concatenate(real, axis=1), jnp.concatenate(imag, axis=1)], axis=0)
        field = mm(pair(turn_ref), split(stack))
        field_ref[c] = field
        light = jnp.zeros((GRID, GRID), f32)
        for s in range(own):
            re = field[:GRID, s * GRID : (s + 1) * GRID]
            im = field[GRID:, s * GRID : (s + 1) * GRID]
            light = light + weights[s] * (re * re + im * im)
        return light

    def owning_sum(k):
        def owning(condition, action):
            if owners == n:
                action()
            else:
                pl.when(condition)(action)

        def scatter(peer):
            return pltpu.make_async_remote_copy(
                src_ref=part_ref.at[k, lax.rem(peer, owners)],
                dst_ref=gather_ref.at[k, me],
                send_sem=send_sem.at[2 * k, peer],
                recv_sem=recv_sem.at[2 * k, me],
                device_id={"src": peer},
                device_id_type=MESH,
            )

        def arrival(peer):
            return pltpu.make_async_remote_copy(
                src_ref=part_ref.at[k, 0],
                dst_ref=gather_ref.at[k, peer],
                send_sem=send_sem.at[2 * k, peer],
                recv_sem=recv_sem.at[2 * k, peer],
                device_id={"src": peer},
                device_id_type=MESH,
            )

        def share(peer):
            return pltpu.make_async_remote_copy(
                src_ref=total_ref.at[k, lax.rem(me, owners)],
                dst_ref=total_ref.at[k, lax.rem(me, owners)],
                send_sem=send_sem.at[2 * k + 1, peer],
                recv_sem=recv_sem.at[2 * k + 1, me],
                device_id={"src": peer},
                device_id_type=MESH,
            )

        def shared(peer):
            return pltpu.make_async_remote_copy(
                src_ref=total_ref.at[k, lax.rem(peer, owners)],
                dst_ref=total_ref.at[k, lax.rem(peer, owners)],
                send_sem=send_sem.at[2 * k + 1, peer],
                recv_sem=recv_sem.at[2 * k + 1, peer],
                device_id={"src": peer},
                device_id_type=MESH,
            )

        def other(i):
            return lax.rem(me + i + 1, n)

        def begin(value):
            for p in range(owners):
                part_ref[k, p] = value[p * held : (p + 1) * held]
            each(n - 1, lambda i: owning(other(i) < owners, lambda: scatter(other(i)).start()))

        def add_up():
            each(n - 1, lambda i: arrival(other(i)).wait_recv())
            gather_ref[k, me] = part_ref[k, lax.rem(me, owners)]
            block = gather_ref[k, 0]
            if n <= 16:
                for p in range(1, n):
                    block = block + gather_ref[k, p]
            else:
                block = lax.fori_loop(1, n, lambda p, t: t + gather_ref[k, p], block)
            total_ref[k, lax.rem(me, owners)] = block
            each(n - 1, lambda i: share(other(i)).start())

        def middle():
            owning(me < owners, add_up)

        def end():
            each(n - 1, lambda i: owning(other(i) < owners, lambda: shared(other(i)).wait_recv()))
            return jnp.concatenate([total_ref[k, p] for p in range(owners)], axis=0)

        def drain():
            each(n - 1, lambda i: owning(other(i) < owners, lambda: scatter(other(i)).wait_send()))
            owning(me < owners, lambda: each(n - 1, lambda i: share(other(i)).wait_send()))

        return begin, middle, end, drain

    sums = [owning_sum(k) for k in range(2 * tiles)]
    for c in range(tiles):
        sums[c][0](image(c))

    weight = weight_ref[0]
    for s in range(1, n * own):
        weight = weight + weight_ref[s]
    inverse = 1.0 / jnp.full((1, TS), weight, f32)
    for load in loads[7:]:
        load.wait()
    core = pair(core_ref)
    coret = pair(coret_ref)
    lead = split(turns().T)
    for c in range(tiles):
        sums[c][1]()

    def pulled(c, light):
        up_ref[c] = mm(core, split(light))
        pull_ref[c] = jnp.zeros((GRID, GRID), f32)

        def resist(i, carry):
            at = pl.multiple_of(i * CHUNK, CHUNK)
            fine = mm(split(up_ref[c, pl.ds(at, CHUNK), :]), coret)
            slope = resist_slope(fine * inverse, target_ref[pl.ds(at, CHUNK), c * TS : (c + 1) * TS]) * inverse
            rows = mm(split(slope), core)
            pull_ref[c] += mm(pair(coret_ref, slice(None), pl.ds(at, CHUNK)), split(rows))
            return carry

        lax.fori_loop(0, TS // CHUNK, resist, 0)
        return pull_ref[c]

    def gradient(c, pull):
        pull = jnp.concatenate([pull] * 2, axis=0)
        pull = jnp.concatenate([pull * (2.0 * w) for w in weights], axis=1)
        u = mm(pair(turnt_ref), split(field_ref[c] * pull))
        rows = []
        for s in range(own):
            re = u[:freqs, s * GRID : (s + 1) * GRID]
            im = u[freqs:, s * GRID : (s + 1) * GRID]
            rows.append(jnp.concatenate([re, im], axis=1))
            rows.append(jnp.concatenate([im, -re], axis=1))
        back = mm(split(jnp.concatenate(rows, axis=0)), fixed, NT) * scaled
        lows = []
        for s in range(own):
            wide = mm(split(back[2 * s * freqs : 2 * (s + 1) * freqs]), split(shifted_ref[s, 1]))
            real, imag = halves(wide, 1, freqs)
            lows += [real[0], -imag[0]]
        return mm(lead, split(jnp.concatenate(lows, axis=0)))

    for c in range(tiles):
        sums[tiles + c][0](gradient(c, pulled(c, sums[c][2]())))
    for c in range(tiles):
        sums[tiles + c][1]()
    grid_grad = split(jnp.concatenate([sums[tiles + c][2]() for c in range(tiles)], axis=1))
    at = pl.multiple_of(me * width, width)
    block = split(mm(grid_grad, pair(across_ref, pl.ds(at, width)), NT))
    rim_ref[...] = mm(pair(edge_ref, side), block)
    rim = pltpu.make_async_remote_copy(
        src_ref=rim_ref,
        dst_ref=rimin_ref,
        send_sem=rim_sem.at[0],
        recv_sem=rim_sem.at[1],
        device_id={"tile": 1 - side},
        device_id_type=MESH,
    )
    rim.start()
    out_ref[...] = mm(core, block)
    rim.wait_recv()
    out_ref[pl.ds(first, HALO), :] += rimin_ref[...]
    for one in sums:
        one[3]()
    halo.wait_send()
    rim.wait_send()


def shards(mask, target, pupil, source_shift, source_weight):
    n = lax.axis_size("src")
    assert lax.axis_size("tile") == 2
    own = source_shift.shape[0] // n
    freqs = pupil.shape[0]
    columns = mask.shape[1]
    tiles = columns // TS
    width = columns // n
    owners = min(n, GRID // 8)
    spans = tiles * GRID
    spread, across, waves = tables(freqs, columns)
    core = spread[HALO : HALO + TS]
    edges = np.stack([spread[HALO + TS :], spread[:HALO]])
    turn = rotation(waves, freqs)
    constants = [
        two(core), two(core.T), two(across), two(waves),
        two(waves[REACH : REACH + freqs]), two(turn), two(turn.T), two(edges), two(edges.transpose(0, 2, 1)),
    ]
    hbm = pl.BlockSpec(memory_space=pl.ANY)
    vmem = pl.BlockSpec(memory_space=pltpu.VMEM)
    smem = pl.BlockSpec(memory_space=pltpu.SMEM)
    return pl.pallas_call(
        functools.partial(kernel, n, own, freqs, tiles),
        out_shape=jax.ShapeDtypeStruct((TS, width), f32),
        in_specs=[hbm, hbm, vmem, smem, smem] + [hbm] * len(constants),
        out_specs=vmem,
        scratch_shapes=[pltpu.VMEM(c.shape, c.dtype) for c in constants] + [
            pltpu.VMEM((TS, columns), f32),
            pltpu.VMEM((TS, columns), f32),
            pltpu.VMEM((HALO, columns), f32),
            pltpu.VMEM((own, 2, freqs, 2 * GRID), f32),
            pltpu.VMEM((GRID, spans), f32),
            pltpu.VMEM((tiles, 2 * GRID, own * GRID), f32),
            pltpu.VMEM((tiles, TS, GRID), f32),
            pltpu.VMEM((tiles, GRID, GRID), f32),
            pltpu.VMEM((2 * tiles, owners, GRID // owners, GRID), f32),
            pltpu.VMEM((2 * tiles, n, GRID // owners, GRID), f32),
            pltpu.VMEM((2 * tiles, owners, GRID // owners, GRID), f32),
            pltpu.VMEM((HALO, width), f32),
            pltpu.VMEM((HALO, width), f32),
            pltpu.SemaphoreType.DMA((2 + len(constants),)),
            pltpu.SemaphoreType.DMA((2,)),
            pltpu.SemaphoreType.DMA((2,)),
            pltpu.SemaphoreType.DMA((4 * tiles, n)),
            pltpu.SemaphoreType.DMA((4 * tiles, n)),
        ],
        compiler_params=pltpu.CompilerParams(
            collective_id=0, has_side_effects=True, vmem_limit_bytes=60 * 1024 * 1024
        ),
    )(mask, target, pupil, source_shift.T, source_weight, *[jnp.asarray(c) for c in constants])


def solution(mesh):
    placed = (P(("groups", "tile"), None), P(("groups", "tile"), None), P(), P(), P())
    return jax.shard_map(
        shards, mesh=mesh, in_specs=placed, out_specs=P(("groups", "tile"), "src"), check_vma=False
    )
```
